1024 devices in a mesh: section: 128 (over z_lo, x, core), tensor: 8 (over z_hi, y).
Axes of the slice: x: 4, y: 4, z: 32 (z_hi: 2, z_lo: 16; z = z_hi * 16 + z_lo), core: 2. Of those that a mesh axis runs over, the one named last changes fastest.
Arguments:
- x_sent: bfloat16 [128, 128, 8192], P('section', None, 'tensor'), may hold values from -6 to 6
- grad_in: bfloat16 [128, 128, 8192], P('section', None, 'tensor'), may hold values from -4 to 4
- norm_gain: float32 [128, 8192], P('section', 'tensor'), may hold values from 0.25 to 1.75
- w_key: bfloat16 [128, 8192, 1024], P('section', 'tensor'), may hold values from -0.0625 to 0.0625
- key_grad: bfloat16 [128, 128, 1024], P('section'), may hold values from -6 to 6
- held_in: bfloat16 [128, 128, 8192], P('section', None, 'tensor'), may hold values from -1 to 1
- held_scale: float32 [128, 128, 64], P('section', None, 'tensor'), may hold values from 0.25 to 4
- stash_flags: int32 [128, 2], replicated, may hold values from 0 to 1, as said below
Outputs:
- key_rows: bfloat16 [128, 128, 1024], P('section', 'tensor')
- held_out: bfloat16 [128, 128, 8192], P('section', None, 'tensor')
- scale_out: float32 [128, 128, 64], P('section', None, 'tensor')
- grad_out: bfloat16 [128, 128, 8192], P('section', None, 'tensor')
The draws below stay inside these ranges and needn't reach their ends.
Inputs may be any that keep to these rules, and one draw needn't show every extreme that they name: stash_flags[s, c] == stash_flags[127 - s, c]; in each column some mirror pair has flag 1 and some has flag 0.
All inputs are finite; a program needn't handle non-finite values. Where the reference program divides by a largest or mean magnitude, that divisor is 1e-20 or more.
Results may differ from the reference program's by a relative error of at most 0.013.
Values may be sent and summed in bfloat16 or wider, within the bound.
A program may use at most 32 MiB of HBM per device.

```python
import math
import jax
import jax.numpy as jnp
from jax import lax

D = 8192
TOK = 128
BLOCK = 128
SECTIONS = 128
KVD = 1024
NBLK = 64


def flag_column(key, half_count):
    key_bits, key_pick, key_other = jax.random.split(key, 3)
    coins = jax.random.randint(key_bits, (half_count,), 0, 2).astype(jnp.int32)
    chosen_one = jax.random.randint(key_pick, (), 0, half_count)
    chosen_zero = (chosen_one + 1 + jax.random.randint(key_other, (), 0, half_count - 1)) % half_count
    places = jnp.arange(half_count)
    coins = jnp.where(places == chosen_one, 1, coins)
    coins = jnp.where(places == chosen_zero, 0, coins)
    return jnp.concatenate([coins, coins[::-1]]).astype(jnp.int32)


def draw_stash_flags(key, part):
    half_count = SECTIONS // 2
    first = flag_column(jax.random.fold_in(key, 11), half_count)
    second = flag_column(jax.random.fold_in(key, 23), half_count)
    return jnp.stack([first, second], axis=1)


def levels(rng, extent, cuts, low, high):
    factor_of = 1.0
    for dim, shards_of in cuts:
        heights = jax.random.uniform(jax.random.fold_in(jax.random.fold_in(rng, 6), dim), (shards_of,), jnp.float32, low / len(cuts), high / len(cuts))
        factor_of = factor_of * jnp.repeat(jnp.exp(heights), extent[dim] // shards_of).reshape((-1,) + (1,) * (len(extent) - 1 - dim))
    return factor_of


def bell_draw(own_key, shape, deviation, bound, cuts=(), kind=jnp.bfloat16):
    gain = levels(own_key, shape, cuts, -0.22, 0.18) if cuts else 1.0
    array = jax.random.normal(own_key, shape, jnp.float32) * deviation * gain
    return jnp.minimum(jnp.maximum(array, -bound), bound).astype(kind)


def setup_inputs(seed: int = 0) -> dict:
    splits = jax.random.split(jax.random.key(seed), 9)
    x_sent = bell_draw(splits[0], (SECTIONS, TOK, D), 1.0, 6.0, ((0, 128), (2, 8)))
    grad_in = bell_draw(splits[1], (SECTIONS, TOK, D), 0.5, 4.0, ((0, 128), (2, 8)))
    norm_gain = jnp.clip(1.0 + 0.15 * jax.random.normal(splits[2], (SECTIONS, D), jnp.float32), 0.25, 1.75)
    w_key = bell_draw(splits[3], (SECTIONS, D, KVD), D ** -0.5, 0.0625, ((0, 128), (1, 8)))
    key_grad = bell_draw(splits[4], (SECTIONS, TOK, KVD), 1.0, 6.0, ((0, 128),))
    held_in = jnp.clip(jax.random.uniform(splits[5], (SECTIONS, TOK, D), jnp.float32, -1.0, 1.0) * levels(splits[5], (SECTIONS, TOK, D), ((0, 128), (2, 8)), -0.4, 0.0), -1.0, 1.0).astype(jnp.bfloat16)
    held_scale = jnp.clip(jnp.exp(math.log(4.0) - 2.7725887 * jax.random.uniform(splits[6], (SECTIONS, TOK, NBLK), jnp.float32) ** levels(splits[6], (SECTIONS, TOK, NBLK), ((0, 128), (2, 8)), -0.2, 0.2)), 0.25, 4.0)
    stash_flags = draw_stash_flags(jax.random.fold_in(splits[8], 71), 0)
    return {"x_sent": x_sent, "grad_in": grad_in, "norm_gain": norm_gain, "w_key": w_key, "key_grad": key_grad, "held_in": held_in, "held_scale": held_scale, "stash_flags": stash_flags}


epsilon_norm = 1e-05
epsilon_scale = 1e-06

def normalize(values, gain_row):
    mean_sq = lax.optimization_barrier(jnp.mean(values * values, axis=-1, keepdims=True))
    inverse = lax.rsqrt(mean_sq + epsilon_norm)
    return (values * inverse * gain_row, inverse)

def quantize(values):
    blocks = values.reshape(values.shape[:-1] + (D // BLOCK, BLOCK))
    block_scale = lax.optimization_barrier(jnp.max(jnp.abs(blocks), axis=-1)) + epsilon_scale
    packed = (blocks / block_scale[..., None]).astype(jnp.bfloat16)
    return (packed.reshape(values.shape), block_scale)

def restore(packed, block_scale):
    blocks = packed.astype(jnp.float32).reshape(packed.shape[:-1] + (D // BLOCK, BLOCK))
    return (blocks * block_scale[..., None]).reshape(packed.shape)

def section_keys(pair):
    normed, weight = pair
    return jnp.dot(normed, weight, preferred_element_type=jnp.float32).astype(jnp.bfloat16)

def section_normed_grad(pair):
    gradient, weight = pair
    return lax.dot_general(gradient, weight, (((1,), (1,)), ((), ())), preferred_element_type=jnp.float32)

def reference(x_sent, grad_in, norm_gain, w_key, key_grad, held_in, held_scale, stash_flags):
    arrived = jnp.roll(x_sent, 1, axis=0).astype(jnp.float32)
    downward = jnp.roll(grad_in, -1, axis=0).astype(jnp.float32)
    gain_rows = norm_gain[:, None, :]
    normed = normalize(arrived, gain_rows)[0].astype(jnp.bfloat16)
    key_rows = lax.map(section_keys, (normed, w_key))
    new_stash, new_scale = quantize(arrived)
    fetched = (stash_flags[:, 0] == 1)[:, None, None]
    parked = (stash_flags[:, 1] == 1)[:, None, None]
    held_out = jnp.where(parked, jnp.flip(new_stash, 0), new_stash)
    scale_out = jnp.where(parked, jnp.flip(new_scale, 0), new_scale)
    source_q = jnp.where(fetched, jnp.flip(held_in, 0), held_in)
    source_s = jnp.where(fetched, jnp.flip(held_scale, 0), held_scale)
    saved = restore(source_q, source_s)
    dnormed = lax.map(section_normed_grad, (key_grad, w_key))
    _, inverse = normalize(saved, gain_rows)
    scaled = gain_rows * dnormed
    input_grad = inverse * scaled - saved * inverse ** 3 * lax.optimization_barrier(jnp.mean(saved * scaled, axis=-1, keepdims=True))
    grad_out = (downward + input_grad).astype(jnp.bfloat16)
    return (key_rows, held_out, scale_out, grad_out)
```

```python
import functools

import jax
import jax.numpy as jnp
from jax import lax
from jax.experimental import pallas as pl
from jax.experimental.pallas import tpu as pltpu
from jax.sharding import PartitionSpec as P

MESH = pl.DeviceIdType.MESH
BLOCK = 128
ROW = 8
HALVES = 2
CHUNKS = 4

epsilon_norm = 1e-05
epsilon_scale = 1e-06

XS, GS, HELD, SCALE, XM = 0, 1, 2, 3, 4


def column_form(rows8):
    return jnp.concatenate([rows8] * 16, axis=0).T


def kernel(
    sizes,
    x_hbm, g_hbm, gain_hbm, w_hbm, kg_hbm, held_hbm, hs_hbm, flags_hbm,
    key_v, held_v, scale_v, grad_v,
    gain, w, kg, held, hs, flags,
    arr, down, rheld, rhs, xm,
    scaled, saved, yb, ss, kpf, kp, kss, ky, kys, kz_src, kzs_src, kz, kzs,
    sums, sy, sz_src, sz, sc_cols,
    lsem, send, recv, chain, token,
):
    sections, tensors, tok, feats, width = sizes
    ys, zlo = tensors // HALVES, sections // ROW
    zs = HALVES * zlo
    rt = tok // tensors
    nblk = feats // BLOCK
    crow = tok // CHUNKS
    f32 = jnp.float32

    s = lax.axis_index("section")
    t = lax.axis_index("tensor")
    r, lo = s % ROW, s // ROW
    hi, y = t // ys, t % ys
    z = hi * zlo + lo

    def at_z(step):
        there = (z + step + zs) % zs
        return ((there % zlo) * ROW + r, (there // zlo) * ys + y)

    def y_peer(k):
        return (s, hi * ys + (y + k) % ys)

    z_peer = (s, (1 - hi) * ys + y)
    nxt = ((s + 1) % sections, t)
    prv = ((s + sections - 1) % sections, t)
    mirror = (sections - 1 - s, t)
    mirror_x = ((2 * sections - 2 - s) % sections, t)
    own_x = mirror_x[0] == s

    locals_in = [
        pltpu.make_async_copy(a, b, lsem.at[i])
        for i, (a, b) in enumerate(
            ((w_hbm, w), (kg_hbm, kg), (gain_hbm, gain), (held_hbm, held), (hs_hbm, hs), (flags_hbm, flags))
        )
    ]
    for copy in locals_in:
        copy.start()

    def remote(number, src, dst, device):
        return pltpu.make_async_remote_copy(
            src_ref=src, dst_ref=dst, send_sem=send.at[number], recv_sem=recv.at[number],
            device_id=device, device_id_type=MESH,
        )

    x_copy = remote(XS, x_hbm, arr, nxt)
    g_copy = remote(GS, g_hbm, down, prv)
    h_copy = remote(HELD, held_hbm, rheld, mirror)
    hs_copy = remote(SCALE, hs_hbm, rhs, mirror)

    def x_rows(c):
        return x_hbm.at[pl.ds(c * crow, crow)], xm.at[pl.ds(c * crow, crow)]

    xm_copies = [remote(XM + c, *x_rows(c), mirror_x) for c in range(CHUNKS)]
    xm_own = [pltpu.make_async_copy(*x_rows(c), recv.at[XM + c]) for c in range(CHUNKS)]
    n = XM + CHUNKS
    ky_copies = [remote(n + k - 1, kp.at[(y + k) % ys], ky.at[k - 1], y_peer(k)) for k in range(1, ys)]
    n += ys - 1
    kys_copies = [remote(n + k - 1, kss.at[(y + k) % ys], kys.at[k - 1], y_peer(k)) for k in range(1, ys)]
    n += ys - 1
    kz_copy = remote(n, kz_src, kz, z_peer)
    kzs_copy = remote(n + 1, kzs_src, kzs, z_peer)
    n += 2
    sy_copies = [remote(n + k - 1, sums, sy.at[k - 1], y_peer(k)) for k in range(1, ys)]
    n += ys - 1
    sz_copy = remote(n, sz_src, sz, z_peer)

    def issue(stage):
        for copies, target in (((x_copy,), nxt), ((g_copy,), prv), ((hs_copy, h_copy), mirror)):
            apart = jnp.abs(target[0] // ROW - lo)
            first = jnp.where(apart > 0, 1, 0)
            for k in range(1, steps):
                first = jnp.where(apart >= 1 << k, k + 1, first)

            @pl.when(first == stage)
            def _():
                for copy in copies:
                    copy.start()

    steps = zlo.bit_length() - 1
    barrier = pltpu.get_barrier_semaphore()
    near = [(lo * ROW + (r + k) % ROW, t) for k in range(1, ROW)]
    near += [y_peer(k) for k in range(1, ys)] + [at_z(1), at_z(-1)]
    for device in near:
        pl.semaphore_signal(barrier, inc=1, device_id=device, device_id_type=MESH)
    pl.semaphore_wait(barrier, len(near))
    issue(0)
    for k in range(steps):
        for way in range(2):
            there = at_z((1 - 2 * way) << k)
            pl.semaphore_signal(chain.at[2 * k + way], inc=1, device_id=there, device_id_type=MESH)
        pl.semaphore_wait(chain.at[2 * k], 1)
        pl.semaphore_wait(chain.at[2 * k + 1], 1)
        issue(k + 1)

    for copy in locals_in:
        copy.wait()

    for c in range(0, feats, 256):
        cols = pl.ds(c, min(256, feats))
        part = lax.dot_general(
            kg[...], w[cols, :], (((1,), (1,)), ((), ())), preferred_element_type=f32
        )
        scaled[:, cols] = part * gain[:, cols]

    x_copy.wait_recv()
    total = jnp.zeros((tok, BLOCK), f32)
    for b in range(nblk):
        cols = pl.ds(b * BLOCK, BLOCK)
        v = arr[:, cols].astype(f32)
        total += v * v
        yb[:, cols] = (v * gain[:, cols]).astype(jnp.bfloat16)
    ss[...] = total
    for c in range(0, width, 256):
        cols = pl.ds(c, min(256, width))
        kpf[:, cols] = jnp.dot(yb[...], w[:, cols], preferred_element_type=f32)
    for yy in range(ys):
        for side in range(HALVES):
            half = hi if side == 0 else 1 - hi
            rows = pl.ds(pl.multiple_of((half * ys + yy) * rt, rt), rt)
            here = pl.ds(side * rt, rt)
            kp[yy, here, :] = kpf[rows, :].astype(jnp.bfloat16)
            kss[yy, here, :] = ss[rows, :]
    for copy in ky_copies + kys_copies:
        copy.start()
    for copy in ky_copies + kys_copies:
        copy.wait_recv()
    sides = []
    for side in range(HALVES):
        half = hi if side == 0 else 1 - hi
        rows = pl.ds(pl.multiple_of((half * ys + y) * rt, rt), rt)
        here = pl.ds(side * rt, rt)
        key_sum, sq_sum = kpf[rows, :], ss[rows, :]
        for k in range(ys - 1):
            key_sum = key_sum + ky[k, here, :].astype(f32)
            sq_sum = sq_sum + kys[k, here, :]
        sides.append((rows, key_sum, sq_sum))
    kz_src[...] = sides[1][1].astype(jnp.bfloat16)
    kzs_src[...] = sides[1][2]
    kz_copy.start()
    kzs_copy.start()
    own_rows = sides[0][0]
    kpf[own_rows, :] = sides[0][1]
    ss[own_rows, :] = sides[0][2]

    lane = lax.broadcasted_iota(jnp.int32, (2, sections), 1)
    mine = jnp.sum(jnp.where(lane == s, flags[...].astype(f32), 0.0), axis=1, keepdims=True)
    fetched, parked = mine[0:1, :], mine[1:2, :]

    hs_copy.wait_recv()
    h_copy.wait_recv()

    pick = jnp.broadcast_to(fetched, (tok, BLOCK)) > 0.5
    scales = column_form(jnp.where(jnp.broadcast_to(fetched, hs.shape) > 0.5, rhs[...], hs[...]))
    square = jnp.zeros((tok, BLOCK), f32)
    cross = jnp.zeros((tok, BLOCK), f32)
    for b in range(nblk):
        cols = pl.ds(b * BLOCK, BLOCK)
        v = jnp.where(pick, rheld[:, cols].astype(f32), held[:, cols].astype(f32))
        v = v * scales[:, b : b + 1]
        saved[:, cols] = v
        square += v * v
        cross += v * scaled[:, cols]
    lane = lax.broadcasted_iota(jnp.int32, (tok, BLOCK), 1)
    square = jnp.sum(square, axis=1, keepdims=True)
    cross = jnp.sum(cross, axis=1, keepdims=True)
    sums[...] = jnp.where(lane == 0, square, jnp.where(lane == 1, cross, 0.0)).T[:8, :]
    for copy in sy_copies:
        copy.start()
    for copy in sy_copies:
        copy.wait_recv()
    total = sums[...]
    for k in range(ys - 1):
        total = total + sy[k]
    sz_src[...] = total
    sz_copy.start()

    low = lo < zlo // 2

    @pl.when(jnp.logical_and(lo != zlo // 2 - 1, lo != zlo // 2))
    def _():
        pl.semaphore_wait(token, 1)

    @pl.when(jnp.logical_and(low, lo > 0))
    def _():
        pl.semaphore_signal(token, inc=1, device_id=at_z(-1), device_id_type=MESH)

    @pl.when(jnp.logical_and(jnp.logical_not(low), lo < zlo - 1))
    def _():
        pl.semaphore_signal(token, inc=1, device_id=at_z(1), device_id_type=MESH)

    @pl.when(own_x)
    def _():
        for copy in xm_own:
            copy.start()

    @pl.when(jnp.logical_not(own_x))
    def _():
        for copy in xm_copies:
            copy.start()

    kz_copy.wait_recv()
    kzs_copy.wait_recv()
    full = feats * tensors
    squares = jnp.sum(ss[own_rows, :] + kzs[...], axis=1, keepdims=True)
    inverse = lax.rsqrt(squares / full + epsilon_norm)
    key_v[...] = ((kpf[own_rows, :] + kz[...].astype(f32)) * inverse).astype(jnp.bfloat16)

    sz_copy.wait_recv()
    g_copy.wait_recv()
    totals = column_form(sz_src[...] + sz[...])
    inverse = lax.rsqrt(totals[:, 0:1] / full + epsilon_norm)
    factor = inverse * inverse * inverse * (totals[:, 1:2] / full)
    for b in range(nblk):
        cols = pl.ds(b * BLOCK, BLOCK)
        v = inverse * scaled[:, cols] - saved[:, cols] * factor
        grad_v[:, cols] = (down[:, cols].astype(f32) + v).astype(jnp.bfloat16)

    pick = jnp.broadcast_to(parked, (crow, BLOCK)) > 0.5
    lane = lax.broadcasted_iota(jnp.int32, (crow, BLOCK), 1)
    for c in range(CHUNKS):

        @pl.when(own_x)
        def _():
            xm_own[c].wait()

        @pl.when(jnp.logical_not(own_x))
        def _():
            xm_copies[c].wait_recv()

        rows = pl.ds(c * crow, crow)
        columns = jnp.zeros((crow, BLOCK), f32)
        for b in range(nblk):
            cols = pl.ds(b * BLOCK, BLOCK)
            v = jnp.where(pick, xm[rows, cols].astype(f32), arr[rows, cols].astype(f32))
            scale = jnp.max(jnp.abs(v), axis=1, keepdims=True) + epsilon_scale
            held_v[rows, cols] = (v / scale).astype(jnp.bfloat16)
            columns = jnp.where(lane == b, scale, columns)
        sc_cols[rows, :] = columns
    scale_v[...] = sc_cols[...].T[:8, :]

    for copy in [x_copy, g_copy, h_copy, hs_copy, kz_copy, kzs_copy, sz_copy] + ky_copies + kys_copies + sy_copies:
        copy.wait_send()

    @pl.when(jnp.logical_not(own_x))
    def _():
        for copy in xm_copies:
            copy.wait_send()


def flush(*refs):
    sources, targets, sem = refs[:4], refs[4:8], refs[8]
    copies = [pltpu.make_async_copy(a, b, sem.at[i]) for i, (a, b) in enumerate(zip(sources, targets))]
    for copy in copies:
        copy.start()
    for copy in copies:
        copy.wait()


def on_device(x_sent, grad_in, norm_gain, w_key, key_grad, held_in, held_scale, stash_flags):
    sections, tensors = lax.axis_size("section"), lax.axis_size("tensor")
    tok, feats = x_sent.shape[1:]
    width = w_key.shape[2]
    nblk = feats // BLOCK
    ys, zlo = tensors // HALVES, sections // ROW
    rt = tok // tensors
    bf16, f32 = jnp.bfloat16, jnp.float32
    v, dma = pltpu.VMEM, pltpu.SemaphoreType.DMA
    hs = held_scale[0].T
    copies = XM + CHUNKS + 3 * (ys - 1) + 3
    shapes = (((rt, width), bf16), ((tok, feats), bf16), ((nblk, tok), f32), ((tok, feats), bf16))
    here = pl.pallas_call(
        functools.partial(kernel, (sections, tensors, tok, feats, width)),
        out_shape=[v(*shape) for shape in shapes],
        in_specs=[pl.BlockSpec(memory_space=pltpu.HBM)] * 8,
        out_specs=[pl.BlockSpec(memory_space=v)] * 4,
        scratch_shapes=[
            v((1, feats), f32), v((feats, width), bf16), v((tok, width), bf16),
            v((tok, feats), bf16), v((nblk, tok), f32), v((2, sections), jnp.int32),
            v((tok, feats), bf16), v((tok, feats), bf16), v((tok, feats), bf16),
            v((nblk, tok), f32), v((tok, feats), bf16),
            v((tok, feats), f32), v((tok, feats), f32), v((tok, feats), bf16),
            v((tok, BLOCK), f32), v((tok, width), f32),
            v((ys, HALVES * rt, width), bf16), v((ys, HALVES * rt, BLOCK), f32),
            v((max(ys - 1, 1), HALVES * rt, width), bf16), v((max(ys - 1, 1), HALVES * rt, BLOCK), f32),
            v((rt, width), bf16), v((rt, BLOCK), f32), v((rt, width), bf16), v((rt, BLOCK), f32),
            v((8, tok), f32), v((max(ys - 1, 1), 8, tok), f32), v((8, tok), f32), v((8, tok), f32),
            v((tok, BLOCK), f32),
            dma((6,)), dma((copies,)), dma((copies,)),
            pltpu.SemaphoreType.REGULAR((2 * max(zlo.bit_length() - 1, 1),)), pltpu.SemaphoreType.REGULAR,
        ],
        compiler_params=pltpu.CompilerParams(
            collective_id=0, has_side_effects=True, vmem_limit_bytes=24 * 1024 * 1024
        ),
        name="tick",
    )(
        *(
            pltpu.with_memory_space_constraint(a, pltpu.HBM)
            for a in (x_sent[0], grad_in[0], norm_gain, w_key[0], key_grad[0], held_in[0], hs, stash_flags.T)
        )
    )
    key, held, scale, grad = pl.pallas_call(
        flush,
        out_shape=[jax.ShapeDtypeStruct(*shape) for shape in shapes],
        in_specs=[pl.BlockSpec(memory_space=v)] * 4,
        out_specs=[pl.BlockSpec(memory_space=pl.ANY)] * 4,
        scratch_shapes=[dma((4,))],
        compiler_params=pltpu.CompilerParams(vmem_limit_bytes=8 * 1024 * 1024),
        name="flush",
    )(*here)
    return key[None], held[None], scale.T[None], grad[None]


def solution(mesh):
    return jax.shard_map(
        on_device,
        mesh=mesh,
        in_specs=(
            P("section", None, "tensor"),
            P("section", None, "tensor"),
            P("section", "tensor"),
            P("section", "tensor", None),
            P("section", None, None),
            P("section", None, "tensor"),
            P("section", None, "tensor"),
            P(),
        ),
        out_specs=(
            P("section", "tensor", None),
            P("section", None, "tensor"),
            P("section", None, "tensor"),
            P("section", None, "tensor"),
        ),
        check_vma=False,
    )
```

```python
import functools

import jax
import jax.numpy as jnp
from jax import lax
from jax.experimental import pallas as pl
from jax.experimental.pallas import tpu as pltpu
from jax.sharding import PartitionSpec as P

MESH = pl.DeviceIdType.MESH
BLOCK = 128
ROW = 8
HALVES = 2
CHUNKS = 4
FRONT = 1

epsilon_norm = 1e-05
epsilon_scale = 1e-06

XS, GS, HELD, SCALE, XM = 0, 1, 2, 3, 4


def column_form(rows8):
    return jnp.concatenate([rows8] * 16, axis=0).T


def kernel(
    sizes,
    x_hbm, g_hbm, gain_hbm, w_hbm, kg_hbm, held_hbm, hs_hbm, flags_hbm,
    key_v, held_v, scale_v, grad_v,
    gain, w, kg, held, hs, flags,
    arr, down, rheld, rhs, xm,
    scaled, saved, yb, ss, kpf, kp, kss, ky, kys, kz_src, kzs_src, kz, kzs,
    sums, sy, sz_src, sz, sc_cols,
    lsem, send, recv, chain, token, hello,
):
    sections, tensors, tok, feats, width = sizes
    ys, zlo = tensors // HALVES, sections // ROW
    zs = HALVES * zlo
    rt = tok // tensors
    nblk = feats // BLOCK
    crow = tok // CHUNKS
    f32 = jnp.float32

    s = lax.axis_index("section")
    t = lax.axis_index("tensor")
    r, lo = s % ROW, s // ROW
    hi, y = t // ys, t % ys
    z = hi * zlo + lo

    def at_z(step):
        there = (z + step + zs) % zs
        return ((there % zlo) * ROW + r, (there // zlo) * ys + y)

    def y_peer(k):
        return (s, hi * ys + (y + k) % ys)

    z_peer = (s, (1 - hi) * ys + y)
    nxt = ((s + 1) % sections, t)
    prv = ((s + sections - 1) % sections, t)
    mirror = (sections - 1 - s, t)
    mirror_x = ((2 * sections - 2 - s) % sections, t)
    own_x = mirror_x[0] == s

    locals_in = [
        pltpu.make_async_copy(a, b, lsem.at[i])
        for i, (a, b) in enumerate(
            ((w_hbm, w), (kg_hbm, kg), (gain_hbm, gain), (held_hbm, held), (hs_hbm, hs), (flags_hbm, flags))
        )
    ]
    for copy in locals_in:
        copy.start()

    def remote(number, src, dst, device):
        return pltpu.make_async_remote_copy(
            src_ref=src, dst_ref=dst, send_sem=send.at[number], recv_sem=recv.at[number],
            device_id=device, device_id_type=MESH,
        )

    x_copy = remote(XS, x_hbm, arr, nxt)
    g_copy = remote(GS, g_hbm, down, prv)
    h_copy = remote(HELD, held_hbm, rheld, mirror)
    hs_copy = remote(SCALE, hs_hbm, rhs, mirror)

    def x_rows(c):
        return x_hbm.at[pl.ds(c * crow, crow)], xm.at[pl.ds(c * crow, crow)]

    xm_copies = [remote(XM + c, *x_rows(c), mirror_x) for c in range(CHUNKS)]
    xm_own = [pltpu.make_async_copy(*x_rows(c), recv.at[XM + c]) for c in range(CHUNKS)]
    n = XM + CHUNKS
    ky_copies = [remote(n + k - 1, kp.at[(y + k) % ys], ky.at[k - 1], y_peer(k)) for k in range(1, ys)]
    n += ys - 1
    kys_copies = [remote(n + k - 1, kss.at[(y + k) % ys], kys.at[k - 1], y_peer(k)) for k in range(1, ys)]
    n += ys - 1
    kz_copy = remote(n, kz_src, kz, z_peer)
    kzs_copy = remote(n + 1, kzs_src, kzs, z_peer)
    n += 2
    sy_copies = [remote(n + k - 1, sums, sy.at[k - 1], y_peer(k)) for k in range(1, ys)]
    n += ys - 1
    sz_copy = remote(n, sz_src, sz, z_peer)

    low = lo < zlo // 2
    inner = jnp.where(low, zlo // 2 - 1 - lo, lo - zlo // 2)

    @pl.when(own_x)
    def _():
        for copy in xm_own:
            copy.start()

    barrier = pltpu.get_barrier_semaphore()
    last = ROW - 1
    near = [(lo * ROW + (r + k) % ROW, t) for k in range(1, ROW)]
    near += [y_peer(k) for k in range(1, ys)] + [at_z(1), at_z(-1)]
    mirror_row = (zlo - 1 - lo) * ROW
    greet = jnp.where(r == 0, last - 1, jnp.where(r == last, 1, last - r))
    for device in near + [(mirror_row + greet, t)]:
        pl.semaphore_signal(barrier, inc=1, device_id=device, device_id_type=MESH)
    first, final = s == 0, s == sections - 1
    to_next = jnp.logical_and(r == last, jnp.logical_not(final))
    to_prev = jnp.logical_and(r == 0, jnp.logical_not(first))
    for crosses, device in ((to_next, nxt), (to_prev, prv)):

        @pl.when(crosses)
        def _():
            pl.semaphore_signal(barrier, inc=1, device_id=device, device_id_type=MESH)

    edge = jnp.logical_or(r == 0, r == last)
    expected = jnp.where(edge, 0, 1) + jnp.where(r == 1, 1, 0) + jnp.where(r == last - 1, 1, 0)
    expected = expected + jnp.where(to_next, 1, 0) + jnp.where(to_prev, 1, 0)
    pl.semaphore_wait(barrier, len(near) + expected)

    @pl.when(jnp.logical_not(final))
    def _():
        x_copy.start()

    @pl.when(jnp.logical_not(first))
    def _():
        g_copy.start()

    @pl.when(r == 1)
    def _():
        pl.semaphore_signal(hello, inc=1, device_id=(lo * ROW, t), device_id_type=MESH)

    @pl.when(r == last - 1)
    def _():
        pl.semaphore_signal(hello, inc=1, device_id=(lo * ROW + last, t), device_id_type=MESH)

    @pl.when(edge)
    def _():
        pl.semaphore_wait(hello, 1)

    @pl.when(final)
    def _():
        x_copy.start()

    hs_copy.start()
    h_copy.start()

    @pl.when(first)
    def _():
        g_copy.start()

    for copy in locals_in:
        copy.wait()

    for c in range(0, feats, 256):
        cols = pl.ds(c, min(256, feats))
        part = lax.dot_general(
            kg[...], w[cols, :], (((1,), (1,)), ((), ())), preferred_element_type=f32
        )
        scaled[:, cols] = part * gain[:, cols]

    for k in range(zlo.bit_length() - 1):
        for way in range(2):
            there = at_z((1 - 2 * way) << k)
            pl.semaphore_signal(chain.at[2 * k + way], inc=1, device_id=there, device_id_type=MESH)
        pl.semaphore_wait(chain.at[2 * k], 1)
        pl.semaphore_wait(chain.at[2 * k + 1], 1)

    x_copy.wait_recv()
    total = jnp.zeros((tok, BLOCK), f32)
    for b in range(nblk):
        cols = pl.ds(b * BLOCK, BLOCK)
        v = arr[:, cols].astype(f32)
        total += v * v
        yb[:, cols] = (v * gain[:, cols]).astype(jnp.bfloat16)
    ss[...] = total
    for c in range(0, width, 256):
        cols = pl.ds(c, min(256, width))
        kpf[:, cols] = jnp.dot(yb[...], w[:, cols], preferred_element_type=f32)
    for yy in range(ys):
        for side in range(HALVES):
            half = hi if side == 0 else 1 - hi
            rows = pl.ds(pl.multiple_of((half * ys + yy) * rt, rt), rt)
            here = pl.ds(side * rt, rt)
            kp[yy, here, :] = kpf[rows, :].astype(jnp.bfloat16)
            kss[yy, here, :] = ss[rows, :]
    for copy in ky_copies + kys_copies:
        copy.start()
    for copy in ky_copies + kys_copies:
        copy.wait_recv()
    sides = []
    for side in range(HALVES):
        half = hi if side == 0 else 1 - hi
        rows = pl.ds(pl.multiple_of((half * ys + y) * rt, rt), rt)
        here = pl.ds(side * rt, rt)
        key_sum, sq_sum = kpf[rows, :], ss[rows, :]
        for k in range(ys - 1):
            key_sum = key_sum + ky[k, here, :].astype(f32)
            sq_sum = sq_sum + kys[k, here, :]
        sides.append((rows, key_sum, sq_sum))
    kz_src[...] = sides[1][1].astype(jnp.bfloat16)
    kzs_src[...] = sides[1][2]
    kz_copy.start()
    kzs_copy.start()
    own_rows = sides[0][0]
    kpf[own_rows, :] = sides[0][1]
    ss[own_rows, :] = sides[0][2]

    lane = lax.broadcasted_iota(jnp.int32, (2, sections), 1)
    mine = jnp.sum(jnp.where(lane == s, flags[...].astype(f32), 0.0), axis=1, keepdims=True)
    fetched, parked = mine[0:1, :], mine[1:2, :]

    hs_copy.wait_recv()
    h_copy.wait_recv()

    @pl.when(jnp.logical_and(inner < FRONT, jnp.logical_not(own_x)))
    def _():
        for copy in xm_copies:
            copy.start()

    pick = jnp.broadcast_to(fetched, (tok, BLOCK)) > 0.5
    scales = column_form(jnp.where(jnp.broadcast_to(fetched, hs.shape) > 0.5, rhs[...], hs[...]))
    square = jnp.zeros((tok, BLOCK), f32)
    cross = jnp.zeros((tok, BLOCK), f32)
    for b in range(nblk):
        cols = pl.ds(b * BLOCK, BLOCK)
        v = jnp.where(pick, rheld[:, cols].astype(f32), held[:, cols].astype(f32))
        v = v * scales[:, b : b + 1]
        saved[:, cols] = v
        square += v * v
        cross += v * scaled[:, cols]
    lane = lax.broadcasted_iota(jnp.int32, (tok, BLOCK), 1)
    square = jnp.sum(square, axis=1, keepdims=True)
    cross = jnp.sum(cross, axis=1, keepdims=True)
    sums[...] = jnp.where(lane == 0, square, jnp.where(lane == 1, cross, 0.0)).T[:8, :]
    for copy in sy_copies:
        copy.start()
    for copy in sy_copies:
        copy.wait_recv()
    total = sums[...]
    for k in range(ys - 1):
        total = total + sy[k]
    sz_src[...] = total
    sz_copy.start()

    @pl.when(inner > 0)
    def _():
        pl.semaphore_wait(token, 1)

    outward = inner < zlo // 2 - 1

    @pl.when(jnp.logical_and(outward, low))
    def _():
        pl.semaphore_signal(token, inc=1, device_id=at_z(-1), device_id_type=MESH)

    @pl.when(jnp.logical_and(outward, jnp.logical_not(low)))
    def _():
        pl.semaphore_signal(token, inc=1, device_id=at_z(1), device_id_type=MESH)

    @pl.when(jnp.logical_and(inner >= FRONT, jnp.logical_not(own_x)))
    def _():
        for copy in xm_copies:
            copy.start()

    kz_copy.wait_recv()
    kzs_copy.wait_recv()
    full = feats * tensors
    squares = jnp.sum(ss[own_rows, :] + kzs[...], axis=1, keepdims=True)
    inverse = lax.rsqrt(squares / full + epsilon_norm)
    key_v[...] = ((kpf[own_rows, :] + kz[...].astype(f32)) * inverse).astype(jnp.bfloat16)

    sz_copy.wait_recv()
    g_copy.wait_recv()
    totals = column_form(sz_src[...] + sz[...])
    inverse = lax.rsqrt(totals[:, 0:1] / full + epsilon_norm)
    factor = inverse * inverse * inverse * (totals[:, 1:2] / full)
    for b in range(nblk):
        cols = pl.ds(b * BLOCK, BLOCK)
        v = inverse * scaled[:, cols] - saved[:, cols] * factor
        grad_v[:, cols] = (down[:, cols].astype(f32) + v).astype(jnp.bfloat16)

    pick = jnp.broadcast_to(parked, (crow, BLOCK)) > 0.5
    lane = lax.broadcasted_iota(jnp.int32, (crow, BLOCK), 1)
    for c in range(CHUNKS):

        @pl.when(own_x)
        def _():
            xm_own[c].wait()

        @pl.when(jnp.logical_not(own_x))
        def _():
            xm_copies[c].wait_recv()

        rows = pl.ds(c * crow, crow)
        columns = jnp.zeros((crow, BLOCK), f32)
        for b in range(nblk):
            cols = pl.ds(b * BLOCK, BLOCK)
            v = jnp.where(pick, xm[rows, cols].astype(f32), arr[rows, cols].astype(f32))
            scale = jnp.max(jnp.abs(v), axis=1, keepdims=True) + epsilon_scale
            held_v[rows, cols] = (v / scale).astype(jnp.bfloat16)
            columns = jnp.where(lane == b, scale, columns)
        sc_cols[rows, :] = columns
    scale_v[...] = sc_cols[...].T[:8, :]

    for copy in [x_copy, g_copy, h_copy, hs_copy, kz_copy, kzs_copy, sz_copy] + ky_copies + kys_copies + sy_copies:
        copy.wait_send()

    @pl.when(jnp.logical_not(own_x))
    def _():
        for copy in xm_copies:
            copy.wait_send()


def flush(*refs):
    sources, targets, sem = refs[:4], refs[4:8], refs[8]
    copies = [pltpu.make_async_copy(a, b, sem.at[i]) for i, (a, b) in enumerate(zip(sources, targets))]
    for copy in copies:
        copy.start()
    for copy in copies:
        copy.wait()


def on_device(x_sent, grad_in, norm_gain, w_key, key_grad, held_in, held_scale, stash_flags):
    sections, tensors = lax.axis_size("section"), lax.axis_size("tensor")
    tok, feats = x_sent.shape[1:]
    width = w_key.shape[2]
    nblk = feats // BLOCK
    ys, zlo = tensors // HALVES, sections // ROW
    rt = tok // tensors
    bf16, f32 = jnp.bfloat16, jnp.float32
    v, dma = pltpu.VMEM, pltpu.SemaphoreType.DMA
    hs = held_scale[0].T
    copies = XM + CHUNKS + 3 * (ys - 1) + 3
    shapes = (((rt, width), bf16), ((tok, feats), bf16), ((nblk, tok), f32), ((tok, feats), bf16))
    here = pl.pallas_call(
        functools.partial(kernel, (sections, tensors, tok, feats, width)),
        out_shape=[v(*shape) for shape in shapes],
        in_specs=[pl.BlockSpec(memory_space=pltpu.HBM)] * 8,
        out_specs=[pl.BlockSpec(memory_space=v)] * 4,
        scratch_shapes=[
            v((1, feats), f32), v((feats, width), bf16), v((tok, width), bf16),
            v((tok, feats), bf16), v((nblk, tok), f32), v((2, sections), jnp.int32),
            v((tok, feats), bf16), v((tok, feats), bf16), v((tok, feats), bf16),
            v((nblk, tok), f32), v((tok, feats), bf16),
            v((tok, feats), f32), v((tok, feats), f32), v((tok, feats), bf16),
            v((tok, BLOCK), f32), v((tok, width), f32),
            v((ys, HALVES * rt, width), bf16), v((ys, HALVES * rt, BLOCK), f32),
            v((max(ys - 1, 1), HALVES * rt, width), bf16), v((max(ys - 1, 1), HALVES * rt, BLOCK), f32),
            v((rt, width), bf16), v((rt, BLOCK), f32), v((rt, width), bf16), v((rt, BLOCK), f32),
            v((8, tok), f32), v((max(ys - 1, 1), 8, tok), f32), v((8, tok), f32), v((8, tok), f32),
            v((tok, BLOCK), f32),
            dma((6,)), dma((copies,)), dma((copies,)),
            pltpu.SemaphoreType.REGULAR((2 * max(zlo.bit_length() - 1, 1),)), pltpu.SemaphoreType.REGULAR, pltpu.SemaphoreType.REGULAR,
        ],
        compiler_params=pltpu.CompilerParams(
            collective_id=0, has_side_effects=True, vmem_limit_bytes=24 * 1024 * 1024
        ),
        name="tick",
    )(
        *(
            pltpu.with_memory_space_constraint(a, pltpu.HBM)
            for a in (x_sent[0], grad_in[0], norm_gain, w_key[0], key_grad[0], held_in[0], hs, stash_flags.T)
        )
    )
    key, held, scale, grad = pl.pallas_call(
        flush,
        out_shape=[jax.ShapeDtypeStruct(*shape) for shape in shapes],
        in_specs=[pl.BlockSpec(memory_space=v)] * 4,
        out_specs=[pl.BlockSpec(memory_space=pl.ANY)] * 4,
        scratch_shapes=[dma((4,))],
        compiler_params=pltpu.CompilerParams(vmem_limit_bytes=8 * 1024 * 1024),
        name="flush",
    )(*here)
    return key[None], held[None], scale.T[None], grad[None]


def solution(mesh):
    return jax.shard_map(
        on_device,
        mesh=mesh,
        in_specs=(
            P("section", None, "tensor"),
            P("section", None, "tensor"),
            P("section", "tensor"),
            P("section", "tensor", None),
            P("section", None, None),
            P("section", None, "tensor"),
            P("section", None, "tensor"),
            P(),
        ),
        out_specs=(
            P("section", "tensor", None),
            P("section", None, "tensor"),
            P("section", None, "tensor"),
            P("section", None, "tensor"),
        ),
        check_vma=False,
    )
```

```python
import functools

import jax
import jax.numpy as jnp
from jax import lax
from jax.experimental import pallas as pl
from jax.experimental.pallas import tpu as pltpu
from jax.sharding import PartitionSpec as P

MESH = pl.DeviceIdType.MESH
BLOCK = 128
ROW = 8
HALVES = 2
CHUNKS = 4
FRONT = 1

epsilon_norm = 1e-05
epsilon_scale = 1e-06

XS, GS, HELD, SCALE, XM = 0, 1, 2, 3, 4


def column_form(rows8):
    return jnp.concatenate([rows8] * 16, axis=0).T


def kernel(
    sizes,
    x_hbm, g_hbm, gain_hbm, w_hbm, kg_hbm, held_hbm, hs_hbm, flags_hbm,
    key_v, held_v, scale_v, grad_v,
    gain, w, kg, held, hs, flags,
    arr, down, rheld, rhs, xm,
    scaled, saved, yb, ss, kpf, kp, kss, ky, kys, kz_src, kzs_src, kz, kzs,
    sums, sy, sz_src, sz, sc_cols,
    lsem, send, recv, chain, token, hello,
):
    sections, tensors, tok, feats, width = sizes
    ys, zlo = tensors // HALVES, sections // ROW
    zs = HALVES * zlo
    rt = tok // tensors
    nblk = feats // BLOCK
    crow = tok // CHUNKS
    f32 = jnp.float32

    s = lax.axis_index("section")
    t = lax.axis_index("tensor")
    r, lo = s % ROW, s // ROW
    hi, y = t // ys, t % ys
    z = hi * zlo + lo

    def at_z(step):
        there = (z + step + zs) % zs
        return ((there % zlo) * ROW + r, (there // zlo) * ys + y)

    def y_peer(k):
        return (s, hi * ys + (y + k) % ys)

    z_peer = (s, (1 - hi) * ys + y)
    nxt = ((s + 1) % sections, t)
    prv = ((s + sections - 1) % sections, t)
    mirror = (sections - 1 - s, t)
    mirror_x = ((2 * sections - 2 - s) % sections, t)
    own_x = mirror_x[0] == s

    locals_in = [
        pltpu.make_async_copy(a, b, lsem.at[i])
        for i, (a, b) in enumerate(
            ((w_hbm, w), (kg_hbm, kg), (gain_hbm, gain), (held_hbm, held), (hs_hbm, hs), (flags_hbm, flags))
        )
    ]
    for copy in locals_in:
        copy.start()

    def remote(number, src, dst, device):
        return pltpu.make_async_remote_copy(
            src_ref=src, dst_ref=dst, send_sem=send.at[number], recv_sem=recv.at[number],
            device_id=device, device_id_type=MESH,
        )

    x_copy = remote(XS, x_hbm, arr, nxt)
    g_copy = remote(GS, g_hbm, down, prv)
    h_copy = remote(HELD, held_hbm, rheld, mirror)
    hs_copy = remote(SCALE, hs_hbm, rhs, mirror)

    def x_rows(c):
        return x_hbm.at[pl.ds(c * crow, crow)], xm.at[pl.ds(c * crow, crow)]

    xm_copies = [remote(XM + c, *x_rows(c), mirror_x) for c in range(CHUNKS)]
    xm_own = [pltpu.make_async_copy(*x_rows(c), recv.at[XM + c]) for c in range(CHUNKS)]
    n = XM + CHUNKS
    ky_copies = [remote(n + k - 1, kp.at[(y + k) % ys], ky.at[k - 1], y_peer(k)) for k in range(1, ys)]
    n += ys - 1
    kys_copies = [remote(n + k - 1, kss.at[(y + k) % ys], kys.at[k - 1], y_peer(k)) for k in range(1, ys)]
    n += ys - 1
    kz_copy = remote(n, kz_src, kz, z_peer)
    kzs_copy = remote(n + 1, kzs_src, kzs, z_peer)
    n += 2
    sy_copies = [remote(n + k - 1, sums, sy.at[k - 1], y_peer(k)) for k in range(1, ys)]
    n += ys - 1
    sz_copy = remote(n, sz_src, sz, z_peer)

    low = lo < zlo // 2
    inner = jnp.where(low, zlo // 2 - 1 - lo, lo - zlo // 2)

    @pl.when(own_x)
    def _():
        for copy in xm_own:
            copy.start()

    barrier = pltpu.get_barrier_semaphore()
    last = ROW - 1
    near = [(lo * ROW + (r + k) % ROW, t) for k in range(1, ROW)]
    near += [y_peer(k) for k in range(1, ys)] + [at_z(1), at_z(-1)]
    mirror_row = (zlo - 1 - lo) * ROW
    greet = jnp.where(r == 0, last - 1, jnp.where(r == last, 1, last - r))
    for device in near + [(mirror_row + greet, t)]:
        pl.semaphore_signal(barrier, inc=1, device_id=device, device_id_type=MESH)
    first, final = s == 0, s == sections - 1
    to_next = jnp.logical_and(r == last, jnp.logical_not(final))
    to_prev = jnp.logical_and(r == 0, jnp.logical_not(first))
    for crosses, device in ((to_next, nxt), (to_prev, prv)):

        @pl.when(crosses)
        def _():
            pl.semaphore_signal(barrier, inc=1, device_id=device, device_id_type=MESH)

    edge = jnp.logical_or(r == 0, r == last)
    expected = jnp.where(edge, 0, 1) + jnp.where(r == 1, 1, 0) + jnp.where(r == last - 1, 1, 0)
    expected = expected + jnp.where(to_next, 1, 0) + jnp.where(to_prev, 1, 0)
    pl.semaphore_wait(barrier, len(near) + expected)

    @pl.when(jnp.logical_not(final))
    def _():
        x_copy.start()

    @pl.when(jnp.logical_not(first))
    def _():
        g_copy.start()

    @pl.when(r == 1)
    def _():
        pl.semaphore_signal(hello, inc=1, device_id=(lo * ROW, t), device_id_type=MESH)

    @pl.when(r == last - 1)
    def _():
        pl.semaphore_signal(hello, inc=1, device_id=(lo * ROW + last, t), device_id_type=MESH)

    @pl.when(edge)
    def _():
        pl.semaphore_wait(hello, 1)

    @pl.when(final)
    def _():
        x_copy.start()

    hs_copy.start()
    h_copy.start()

    @pl.when(first)
    def _():
        g_copy.start()

    for copy in locals_in:
        copy.wait()

    for c in range(0, feats, 256):
        cols = pl.ds(c, min(256, feats))
        part = lax.dot_general(
            kg[...], w[cols, :], (((1,), (1,)), ((), ())), preferred_element_type=f32
        )
        scaled[:, cols] = part * gain[:, cols]

    for k in range(zlo.bit_length() - 1):
        for way in range(2):
            there = at_z((1 - 2 * way) << k)
            pl.semaphore_signal(chain.at[2 * k + way], inc=1, device_id=there, device_id_type=MESH)
        pl.semaphore_wait(chain.at[2 * k], 1)
        pl.semaphore_wait(chain.at[2 * k + 1], 1)

    x_copy.wait_recv()
    total = jnp.zeros((tok, BLOCK), f32)
    for b in range(nblk):
        cols = pl.ds(b * BLOCK, BLOCK)
        v = arr[:, cols].astype(f32)
        total += v * v
        yb[:, cols] = (v * gain[:, cols]).astype(jnp.bfloat16)
    ss[...] = total
    for c in range(0, width, 256):
        cols = pl.ds(c, min(256, width))
        kpf[:, cols] = jnp.dot(yb[...], w[:, cols], preferred_element_type=f32)
    for yy in range(ys):
        for side in range(HALVES):
            half = hi if side == 0 else 1 - hi
            rows = pl.ds(pl.multiple_of((half * ys + yy) * rt, rt), rt)
            here = pl.ds(side * rt, rt)
            kp[yy, here, :] = kpf[rows, :].astype(jnp.bfloat16)
            kss[yy, here, :] = ss[rows, :]
    for copy in ky_copies + kys_copies:
        copy.start()
    for copy in ky_copies + kys_copies:
        copy.wait_recv()
    sides = []
    for side in range(HALVES):
        half = hi if side == 0 else 1 - hi
        rows = pl.ds(pl.multiple_of((half * ys + y) * rt, rt), rt)
        here = pl.ds(side * rt, rt)
        key_sum, sq_sum = kpf[rows, :], ss[rows, :]
        for k in range(ys - 1):
            key_sum = key_sum + ky[k, here, :].astype(f32)
            sq_sum = sq_sum + kys[k, here, :]
        sides.append((rows, key_sum, sq_sum))
    kz_src[...] = sides[1][1].astype(jnp.bfloat16)
    squares = jnp.sum(sides[1][2], axis=1, keepdims=True)
    squares = jnp.broadcast_to(squares, (rt, BLOCK))
    kzs_src[...] = jnp.concatenate([squares] * (BLOCK // rt), axis=0).T[0:1, :]
    kz_copy.start()
    kzs_copy.start()
    own_rows = sides[0][0]
    kpf[own_rows, :] = sides[0][1]
    ss[own_rows, :] = sides[0][2]

    lane = lax.broadcasted_iota(jnp.int32, (2, sections), 1)
    mine = jnp.sum(jnp.where(lane == s, flags[...].astype(f32), 0.0), axis=1, keepdims=True)
    fetched, parked = mine[0:1, :], mine[1:2, :]

    hs_copy.wait_recv()
    h_copy.wait_recv()

    @pl.when(jnp.logical_and(inner < FRONT, jnp.logical_not(own_x)))
    def _():
        for copy in xm_copies:
            copy.start()

    pick = jnp.broadcast_to(fetched, (tok, BLOCK)) > 0.5
    scales = column_form(jnp.where(jnp.broadcast_to(fetched, hs.shape) > 0.5, rhs[...], hs[...]))
    square = jnp.zeros((tok, BLOCK), f32)
    cross = jnp.zeros((tok, BLOCK), f32)
    for b in range(nblk):
        cols = pl.ds(b * BLOCK, BLOCK)
        v = jnp.where(pick, rheld[:, cols].astype(f32), held[:, cols].astype(f32))
        v = v * scales[:, b : b + 1]
        saved[:, cols] = v
        square += v * v
        cross += v * scaled[:, cols]
    lane = lax.broadcasted_iota(jnp.int32, (tok, BLOCK), 1)
    square = jnp.sum(square, axis=1, keepdims=True)
    cross = jnp.sum(cross, axis=1, keepdims=True)
    sums[...] = jnp.where(lane == 0, square, jnp.where(lane == 1, cross, 0.0)).T[:8, :]
    for copy in sy_copies:
        copy.start()
    for copy in sy_copies:
        copy.wait_recv()
    total = sums[...]
    for k in range(ys - 1):
        total = total + sy[k]
    sz_src[...] = total
    sz_copy.start()

    @pl.when(inner > 0)
    def _():
        pl.semaphore_wait(token, 1)

    outward = inner < zlo // 2 - 1

    @pl.when(jnp.logical_and(outward, low))
    def _():
        pl.semaphore_signal(token, inc=1, device_id=at_z(-1), device_id_type=MESH)

    @pl.when(jnp.logical_and(outward, jnp.logical_not(low)))
    def _():
        pl.semaphore_signal(token, inc=1, device_id=at_z(1), device_id_type=MESH)

    @pl.when(jnp.logical_and(inner >= FRONT, jnp.logical_not(own_x)))
    def _():
        for copy in xm_copies:
            copy.start()

    kz_copy.wait_recv()
    kzs_copy.wait_recv()
    full = feats * tensors
    squares = jnp.sum(ss[own_rows, :], axis=1, keepdims=True)
    squares = squares + jnp.broadcast_to(kzs[...], (BLOCK, BLOCK)).T[:rt, 0:1]
    inverse = lax.rsqrt(squares / full + epsilon_norm)
    key_v[...] = ((kpf[own_rows, :] + kz[...].astype(f32)) * inverse).astype(jnp.bfloat16)

    sz_copy.wait_recv()
    g_copy.wait_recv()
    totals = column_form(sz_src[...] + sz[...])
    inverse = lax.rsqrt(totals[:, 0:1] / full + epsilon_norm)
    factor = inverse * inverse * inverse * (totals[:, 1:2] / full)
    for b in range(nblk):
        cols = pl.ds(b * BLOCK, BLOCK)
        v = inverse * scaled[:, cols] - saved[:, cols] * factor
        grad_v[:, cols] = (down[:, cols].astype(f32) + v).astype(jnp.bfloat16)

    pick = jnp.broadcast_to(parked, (crow, BLOCK)) > 0.5
    lane = lax.broadcasted_iota(jnp.int32, (crow, BLOCK), 1)
    for c in range(CHUNKS):

        @pl.when(own_x)
        def _():
            xm_own[c].wait()

        @pl.when(jnp.logical_not(own_x))
        def _():
            xm_copies[c].wait_recv()

        rows = pl.ds(c * crow, crow)
        columns = jnp.zeros((crow, BLOCK), f32)
        for b in range(nblk):
            cols = pl.ds(b * BLOCK, BLOCK)
            v = jnp.where(pick, xm[rows, cols].astype(f32), arr[rows, cols].astype(f32))
            scale = jnp.max(jnp.abs(v), axis=1, keepdims=True) + epsilon_scale
            held_v[rows, cols] = (v / scale).astype(jnp.bfloat16)
            columns = jnp.where(lane == b, scale, columns)
        sc_cols[rows, :] = columns
    scale_v[...] = sc_cols[...].T[:8, :]

    for copy in [x_copy, g_copy, h_copy, hs_copy, kz_copy, kzs_copy, sz_copy] + ky_copies + kys_copies + sy_copies:
        copy.wait_send()

    @pl.when(jnp.logical_not(own_x))
    def _():
        for copy in xm_copies:
            copy.wait_send()


def flush(*refs):
    sources, targets, sem = refs[:4], refs[4:8], refs[8]
    copies = [pltpu.make_async_copy(a, b, sem.at[i]) for i, (a, b) in enumerate(zip(sources, targets))]
    for copy in copies:
        copy.start()
    for copy in copies:
        copy.wait()


def on_device(x_sent, grad_in, norm_gain, w_key, key_grad, held_in, held_scale, stash_flags):
    sections, tensors = lax.axis_size("section"), lax.axis_size("tensor")
    tok, feats = x_sent.shape[1:]
    width = w_key.shape[2]
    nblk = feats // BLOCK
    ys, zlo = tensors // HALVES, sections // ROW
    rt = tok // tensors
    bf16, f32 = jnp.bfloat16, jnp.float32
    v, dma = pltpu.VMEM, pltpu.SemaphoreType.DMA
    hs = held_scale[0].T
    copies = XM + CHUNKS + 3 * (ys - 1) + 3
    shapes = (((rt, width), bf16), ((tok, feats), bf16), ((nblk, tok), f32), ((tok, feats), bf16))
    here = pl.pallas_call(
        functools.partial(kernel, (sections, tensors, tok, feats, width)),
        out_shape=[v(*shape) for shape in shapes],
        in_specs=[pl.BlockSpec(memory_space=pltpu.HBM)] * 8,
        out_specs=[pl.BlockSpec(memory_space=v)] * 4,
        scratch_shapes=[
            v((1, feats), f32), v((feats, width), bf16), v((tok, width), bf16),
            v((tok, feats), bf16), v((nblk, tok), f32), v((2, sections), jnp.int32),
            v((tok, feats), bf16), v((tok, feats), bf16), v((tok, feats), bf16),
            v((nblk, tok), f32), v((tok, feats), bf16),
            v((tok, feats), f32), v((tok, feats), f32), v((tok, feats), bf16),
            v((tok, BLOCK), f32), v((tok, width), f32),
            v((ys, HALVES * rt, width), bf16), v((ys, HALVES * rt, BLOCK), f32),
            v((max(ys - 1, 1), HALVES * rt, width), bf16), v((max(ys - 1, 1), HALVES * rt, BLOCK), f32),
            v((rt, width), bf16), v((1, BLOCK), f32), v((rt, width), bf16), v((1, BLOCK), f32),
            v((8, tok), f32), v((max(ys - 1, 1), 8, tok), f32), v((8, tok), f32), v((8, tok), f32),
            v((tok, BLOCK), f32),
            dma((6,)), dma((copies,)), dma((copies,)),
            pltpu.SemaphoreType.REGULAR((2 * max(zlo.bit_length() - 1, 1),)), pltpu.SemaphoreType.REGULAR, pltpu.SemaphoreType.REGULAR,
        ],
        compiler_params=pltpu.CompilerParams(
            collective_id=0, has_side_effects=True, vmem_limit_bytes=24 * 1024 * 1024
        ),
        name="tick",
    )(
        *(
            pltpu.with_memory_space_constraint(a, pltpu.HBM)
            for a in (x_sent[0], grad_in[0], norm_gain, w_key[0], key_grad[0], held_in[0], hs, stash_flags.T)
        )
    )
    key, held, scale, grad = pl.pallas_call(
        flush,
        out_shape=[jax.ShapeDtypeStruct(*shape) for shape in shapes],
        in_specs=[pl.BlockSpec(memory_space=v)] * 4,
        out_specs=[pl.BlockSpec(memory_space=pl.ANY)] * 4,
        scratch_shapes=[dma((4,))],
        compiler_params=pltpu.CompilerParams(vmem_limit_bytes=8 * 1024 * 1024),
        name="flush",
    )(*here)
    return key[None], held[None], scale.T[None], grad[None]


def solution(mesh):
    return jax.shard_map(
        on_device,
        mesh=mesh,
        in_specs=(
            P("section", None, "tensor"),
            P("section", None, "tensor"),
            P("section", "tensor"),
            P("section", "tensor", None),
            P("section", None, None),
            P("section", None, "tensor"),
            P("section", None, "tensor"),
            P(),
        ),
        out_specs=(
            P("section", "tensor", None),
            P("section", None, "tensor"),
            P("section", None, "tensor"),
            P("section", None, "tensor"),
        ),
        check_vma=False,
    )
```
